768 devices in a mesh: energy: 8 (over y), cell: 96 (over x, z, core).
Axes of the slice: x: 4, y: 8, z: 12, core: 2. Of those that a mesh axis runs over, the one named last changes fastest.
Arguments:
- green_less: float32 [2, 8, 96, 320, 320], P(None, None, 'cell', 'energy'), may hold values from -6 to 6
- green_greater: float32 [2, 8, 96, 320, 320], P(None, None, 'cell', 'energy'), may hold values from -6 to 6
- offsets: int32 [8], replicated, may hold values from 0 to 7, as said below
- orbitals: int32 [96], replicated, may hold values from 192 to 320
- coulomb_diag: float32 [96, 320, 320], P('cell'), may hold values from -0.3125 to 0.3125
- coulomb_up: float32 [96, 320, 320], P('cell'), may hold values from -0.3125 to 0.3125
Outputs:
- screened_diag: float32 [2, 8, 96, 320, 320], P(None, 'energy', 'cell')
- screened_up: float32 [2, 8, 96, 320, 320], P(None, 'energy', 'cell')
The draws below stay inside these ranges and needn't reach their ends.
Inputs may be any that keep to these rules, and one draw needn't show every extreme that they name: offsets is a permutation of 0 to 7.
All inputs are finite; a program needn't handle non-finite values.
Results may differ from the reference program's by a relative error of at most 0.0003.
Values sent between devices are 32-bit elements; how exact they have to be, the bound alone decides.
No kernel may reach another device: no remote copies, remote signals or barrier semaphores. Data moves between devices by JAX's collectives and lax.ppermute only.
A program may use at most 32 MiB of HBM per device.

```python
import math
import jax
import jax.numpy as jnp
from jax import lax

BLK = 320
NE = 8
NC = 96


def draw_offsets(key, part):
    return jax.random.permutation(key, NE).astype(jnp.int32)


def place_ends(entries, key, smallest, largest):
    dims = entries.shape
    spot = [jax.random.randint(jax.random.fold_in(key, axis), (), 0, dims[axis]) for axis in range(len(dims))]
    entries = entries.at[tuple(spot)].set(smallest)
    longest = dims.index(max(dims))
    spot[longest] = (spot[longest] + 1) % dims[longest]
    return entries.at[tuple(spot)].set(largest)


def levels(rng, extent, cuts, low, high):
    level = 1.0
    for position, shards_of in cuts:
        heights = jax.random.uniform(jax.random.fold_in(jax.random.fold_in(rng, 6), position), (shards_of,), jnp.float32, low / len(cuts), high / len(cuts))
        level = level * jnp.repeat(jnp.exp(heights), extent[position] // shards_of).reshape((-1,) + (1,) * (len(extent) - 1 - position))
    return level


def scatter_about(own_key, extent, deviation, limit, cuts=(), kind=jnp.bfloat16):
    drawn = deviation * jax.random.normal(own_key, extent, jnp.float32)
    if cuts:
        drawn = drawn * levels(own_key, extent, cuts, -0.22, 0.18)
    return jnp.clip(drawn, -limit, limit).astype(kind)


def setup_inputs(seed: int = 0) -> dict:
    streams_of = jax.random.split(jax.random.key(seed), 7)
    return {
        "green_less": scatter_about(streams_of[0], (2, NE, NC, BLK, BLK), 1.0, 6.0, ((2, 96), (3, 8)), jnp.float32),
        "green_greater": scatter_about(streams_of[1], (2, NE, NC, BLK, BLK), 1.0, 6.0, ((2, 96), (3, 8)), jnp.float32),
        "offsets": draw_offsets(jax.random.fold_in(streams_of[6], 71), 0),
        "orbitals": place_ends(jax.random.randint(streams_of[3], (NC,), 3 * BLK // 5, BLK + 1), jax.random.fold_in(streams_of[3], 1), 3 * BLK // 5, BLK).astype(jnp.int32),
        "coulomb_diag": scatter_about(streams_of[4], (NC, BLK, BLK), BLK ** -0.5, 0.3125, ((0, 96),), jnp.float32),
        "coulomb_up": scatter_about(streams_of[5], (NC, BLK, BLK), BLK ** -0.5, 0.3125, ((0, 96),), jnp.float32),
    }


HIGH = lax.Precision.HIGHEST

def polarize(lesser, greater, offsets):
    count = lesser.shape[1]
    energies = jnp.arange(count, dtype=jnp.int32)

    def single(shift):
        source = energies - shift
        weight = (source >= 0).astype(jnp.float32)
        picked = jnp.take(greater, jnp.clip(source, 0, count - 1).astype(jnp.int32), axis=1)
        real_part = lesser[0] * picked[0] + lesser[1] * picked[1]
        imag_part = lesser[1] * picked[0] - lesser[0] * picked[1]
        weight = weight.reshape((count,) + (1,) * (lesser.ndim - 2))
        return jnp.stack([lax.optimization_barrier(jnp.sum(real_part * weight, axis=0)), lax.optimization_barrier(jnp.sum(imag_part * weight, axis=0))])
    return lax.map(single, offsets) / math.sqrt(count)

def left_mul(coupling, blocks):
    return jnp.einsum('cij,xcjk->xcik', coupling, blocks, precision=HIGH)

def left_mul_t(coupling, blocks):
    return jnp.einsum('cji,xcjk->xcik', coupling, blocks, precision=HIGH)

def right_mul(blocks, coupling):
    return jnp.einsum('xcij,cjk->xcik', blocks, coupling, precision=HIGH)

def right_mul_t(blocks, coupling):
    return jnp.einsum('xcij,ckj->xcik', blocks, coupling, precision=HIGH)

def screen(polar, vdiag, vup):
    zero_cell = jnp.zeros_like(polar[:, :1])
    zero_block = jnp.zeros_like(vdiag[:1])
    prev_polar = jnp.concatenate([zero_cell, polar[:, :-1]], axis=1)
    next_polar = jnp.concatenate([polar[:, 1:], zero_cell], axis=1)
    prev_up = jnp.concatenate([zero_block, vup[:-1]], axis=0)
    next_diag = jnp.concatenate([vdiag[1:], zero_block], axis=0)
    cells = vdiag.shape[0]
    keep = (jnp.arange(cells, dtype=jnp.int32) < cells - 1).astype(jnp.float32).reshape(1, cells, 1, 1)
    a_here = left_mul(vdiag, polar)
    a_next = left_mul(vup, next_polar)
    diag = right_mul_t(a_here, vdiag) + right_mul_t(a_next, vup) + right_mul(left_mul_t(prev_up, prev_polar), prev_up)
    upper = right_mul(a_here, vup) * keep + right_mul_t(a_next, next_diag)
    return (diag, upper)

def reference(green_less, green_greater, offsets, orbitals, coulomb_diag, coulomb_up):
    rows = jnp.arange(BLK, dtype=jnp.int32)
    inside = (rows[None, :] < orbitals[:, None]).astype(jnp.float32)
    inside_next = (rows[None, :] < jnp.roll(orbitals, -1)[:, None]).astype(jnp.float32)
    vdiag = coulomb_diag * inside[:, :, None] * inside[:, None, :]
    vup = coulomb_up * inside[:, :, None] * inside_next[:, None, :]
    polar = polarize(green_less, green_greater, offsets)

    def per_energy(blocks):
        return screen(blocks, vdiag, vup)
    diag, upper = lax.map(per_energy, polar)
    return (jnp.moveaxis(diag, 0, 1), jnp.moveaxis(upper, 0, 1))
```

```python
import functools
import math

import jax
import jax.numpy as jnp
from jax import lax
from jax.experimental import pallas as pl
from jax.experimental.pallas import tpu as pltpu
from jax.sharding import PartitionSpec as P

F32, BF16 = jnp.float32, jnp.bfloat16
LANES = 128
VMEM = pl.BlockSpec(memory_space=pltpu.VMEM)
SMEM = pl.BlockSpec(memory_space=pltpu.SMEM)


def params(mib):
    return pltpu.CompilerParams(vmem_limit_bytes=mib << 20)


def cost(flops, moved):
    return pl.CostEstimate(flops=flops, bytes_accessed=moved, transcendentals=0)


def shift_cells(block, distance):
    devices = range(lax.axis_size("cell"))
    route = [(i - distance, i) for i in devices if i - distance in devices]
    return lax.ppermute(block, "cell", route)


def lag_products(less, greater, count):
    scale = 1.0 / math.sqrt(count)
    for lag in range(count):
        real = imag = None
        for m in range(lag, count):
            lr, li = less(0, m), less(1, m)
            gr, gi = greater(0, m - lag), greater(1, m - lag)
            re = lr * gr + li * gi
            im = li * gr - lr * gi
            real = re if real is None else real + re
            imag = im if imag is None else imag + im
        yield lag, real * scale, imag * scale


def polar_kernel(first, count, rows, offsets, less, greater, out, slot):
    for n in range(count):
        slot[offsets[n]] = n
    tail = less.shape[-1] % LANES

    def group(g, carry):
        at = pl.ds(pl.multiple_of(g * 8, 8), 8)
        if first:
            columns = pl.ds(LANES, LANES)
        else:
            columns = pl.ds(0, LANES)
        read = lambda ref: (lambda part, m: ref[part, m, 0, at, columns])
        for lag, real, imag in lag_products(read(less), read(greater), count):
            n = slot[lag]
            out[n, 0, at, :] = real
            out[n, 1, at, :] = imag
        if first:
            last = pl.ds(2 * LANES, tail)
            read = lambda ref: (lambda part, m: ref[part, m, 0, at, last])
            for lag, real, imag in lag_products(read(less), read(greater), count):
                out[slot[lag], 2, at, :] = jnp.concatenate([real, imag], axis=-1)
        return carry

    lax.fori_loop(0, rows // 8, group, 0)


def polarize(first, offsets, less, greater):
    _, count, _, rows, width = less.shape
    tiles = 3 if first else 2
    return pl.pallas_call(
        functools.partial(polar_kernel, first, count, rows),
        out_shape=jax.ShapeDtypeStruct((count, tiles, rows, LANES), F32),
        in_specs=[SMEM, VMEM, VMEM],
        out_specs=VMEM,
        scratch_shapes=[pltpu.SMEM((count,), jnp.int32)],
        compiler_params=params(24),
        cost_estimate=cost(36 * 8 * rows * tiles * LANES, 3_000_000),
        name="polar_a" if first else "polar_b",
    )(offsets, less, greater)


def halves(x):
    high = x.astype(BF16)
    return high, (x - high.astype(F32)).astype(BF16)


def dot3(a, b, dims):
    (ah, al), (bh, bl) = a, b
    dot = lambda x, y: lax.dot_general(x, y, (dims, ((), ())), preferred_element_type=F32)
    return dot(ah, bh) + (dot(ah, bl) + dot(al, bh))


NN, NT, TN = ((1,), (0,)), ((1,), (1,)), ((0,), (0,))


def prep_kernel(sizes, diag, up, prev_up, next_diag, diag_o, up_o, prev_o, prevt_o, next_o):
    size = diag.shape[1]
    row = lax.broadcasted_iota(jnp.int32, (size, size), 0)
    col = lax.broadcasted_iota(jnp.int32, (size, size), 1)

    def put(out, x):
        high, low = halves(x)
        out[0], out[1] = high, low

    prev, here, after, after_up = sizes[0], sizes[1], sizes[2], sizes[3]
    put(diag_o, jnp.where((row < here) & (col < here), diag[0], 0.0))
    put(up_o, jnp.where((row < here) & (col < after_up), up[0], 0.0))
    masked = jnp.where((row < prev) & (col < here), prev_up[0], 0.0)
    put(prev_o, masked)
    put(prevt_o, masked.T)
    put(next_o, jnp.where((row < after) & (col < after), next_diag[0], 0.0))


def prepare(sizes, diag, up, prev_up, next_diag):
    size = diag.shape[1]
    out = jax.ShapeDtypeStruct((2, size, size), BF16)
    return pl.pallas_call(
        prep_kernel,
        out_shape=(out,) * 5,
        in_specs=[SMEM] + [VMEM] * 4,
        out_specs=(VMEM,) * 5,
        compiler_params=params(24),
        cost_estimate=cost(8 * 5 * size * size, 5 * 8 * size * size),
        name="prep",
    )(sizes, diag, up, prev_up, next_diag)


def columns_of(tiles):
    return (LANES, 3 * LANES - LANES // 2) if tiles == 3 else (0, LANES)


def block_of(ref):
    src, tiles, rows, lanes = ref.shape
    return jnp.concatenate([ref[:, t].reshape(src * rows, lanes) for t in range(tiles)], axis=1)


def times_block(left, ref):
    product = dot3((left[0], left[1]), halves(block_of(ref)), NN)
    real, imag = product[:, :LANES], product[:, LANES : 2 * LANES]
    if product.shape[1] > 2 * LANES:
        rest, half = product[:, 2 * LANES :], LANES // 2
        real = jnp.concatenate([real, rest[:, :half]], axis=1)
        imag = jnp.concatenate([imag, rest[:, half:]], axis=1)
    return halves(jnp.concatenate([real, imag], axis=0))


def rows_of(ref, lo, hi):
    return ref[0, lo:hi, :], ref[1, lo:hi, :]


def cols_of(ref, lo, hi):
    return ref[0, :, lo:hi], ref[1, :, lo:hi]


def put_sum(out, before, value):
    size = out.shape[-1]
    value = value.reshape(2, size, size)
    for part in range(2):
        out[part] = value[part] if before is None else before[part] + value[part]


def here_kernel(chunk_a, chunk_b, diag, up, diag_out, up_out):
    total_d = total_u = None
    for chunk in (chunk_a, chunk_b):
        lo, hi = columns_of(chunk.shape[1])
        left = times_block(diag, chunk)
        d = dot3(left, cols_of(diag, lo, hi), NT)
        u = dot3(left, rows_of(up, lo, hi), NN)
        total_d = d if total_d is None else total_d + d
        total_u = u if total_u is None else total_u + u
    put_sum(diag_out, None, total_d)
    put_sum(up_out, None, total_u)


def around_kernel(prev_p, next_p, up, prev_up, prev_upt, next_diag, diag_in, up_in, diag_out, up_out):
    lo, hi = columns_of(prev_p.shape[1])
    left = times_block(up, next_p)
    put_sum(up_out, up_in, dot3(left, cols_of(next_diag, lo, hi), NT))
    total = dot3(left, cols_of(up, lo, hi), NT)
    left = times_block(prev_upt, prev_p)
    put_sum(diag_out, diag_in, total + dot3(left, rows_of(prev_up, lo, hi), NN))


def products(kernel, name, operands, size, flops):
    out = jax.ShapeDtypeStruct((2, size, size), F32)
    return pl.pallas_call(
        kernel,
        out_shape=(out, out),
        in_specs=[VMEM] * len(operands),
        out_specs=(VMEM, VMEM),
        compiler_params=params(32),
        cost_estimate=cost(flops, 6_000_000),
        name=name,
    )(*operands)


def per_device(green_less, green_greater, offsets, orbitals, coulomb_diag, coulomb_up):
    size = coulomb_diag.shape[-1]
    cell, cells = lax.axis_index("cell"), lax.axis_size("cell")
    exchange = lambda x: lax.all_to_all(x, "energy", split_axis=0, concat_axis=0, tiled=True)

    chunk_a = exchange(polarize(True, offsets, green_less, green_greater))
    chunk_b = exchange(polarize(False, offsets, green_less, green_greater))
    prev_up = shift_cells(coulomb_up, 1)
    next_diag = shift_cells(coulomb_diag, -1)

    near = orbitals[jnp.clip(cell + jnp.arange(-1, 2, dtype=jnp.int32), 0, cells - 1)]
    last = jnp.where(cell < cells - 1, near[2], 0)
    sizes = jnp.concatenate([near, last[None]])
    diag, up, prev_u, prev_ut, next_d = prepare(sizes, coulomb_diag, coulomb_up, prev_up, next_diag)

    prev_a, next_a = shift_cells(chunk_a, 1), shift_cells(chunk_a, -1)
    prev_b, next_b = shift_cells(chunk_b, 1), shift_cells(chunk_b, -1)
    flops = 2 * 2 * size**3
    d, u = products(here_kernel, "here", (chunk_a, chunk_b, diag, up), size, 9 * flops)
    d, u = products(around_kernel, "around_a", (prev_a, next_a, up, prev_u, prev_ut, next_d, d, u), size, 9 * flops)
    d, u = products(around_kernel, "around_b", (prev_b, next_b, up, prev_u, prev_ut, next_d, d, u), size, 6 * flops)
    return d[:, None, None], u[:, None, None]


def solution(mesh):
    in_specs = (
        P(None, None, "cell", "energy", None),
        P(None, None, "cell", "energy", None),
        P(),
        P(),
        P("cell", None, None),
        P("cell", None, None),
    )
    out_specs = (P(None, "energy", "cell", None, None), P(None, "energy", "cell", None, None))
    return jax.shard_map(
        per_device, mesh=mesh, in_specs=in_specs, out_specs=out_specs, check_vma=False
    )
```
